32 devices in a mesh: row: 2 (over core), col: 16 (over z, y, x).
Axes of the slice: x: 2, y: 2, z: 4, core: 2. Of those that a mesh axis runs over, the one named last changes fastest.
Arguments:
- amplitudes: bfloat16 [2, 1024, 2048], P(None, 'col', 'row'), may hold values from -6 to 6
- integrals: bfloat16 [2, 1024, 8192], P(None, 'row', 'col'), may hold values from -0.125 to 0.125
- amp_screen: int32 [2, 8, 16], P(None, None, 'row'), may hold values 0 or 1
- int_screen: int32 [2, 8, 64], P(None, None, 'col'), may hold values 0 or 1
- residual_in: float32 [2048, 8192], P('row', 'col'), may hold values from -6 to 6
Outputs:
- residual_out: float32 [2048, 8192], P('row', 'col')
The draws below stay inside these ranges and needn't reach their ends.
All inputs are finite; a program needn't handle non-finite values. No bound on the sum of `amp_screen` or of `int_screen` on one device may be relied on, other than what follows from the above.
Results may differ from the reference program's by a relative error of at most 0.0003.
Values may be sent and summed in bfloat16 or wider, within the bound.
No kernel may reach another device: no remote copies, remote signals or barrier semaphores. Data moves between devices by JAX's collectives and lax.ppermute only.
A program may use at most 64 MiB of HBM per device.

```python
import jax
import jax.numpy as jnp

TILE = 128
PANEL = 1024
PAIRS = 2048
AO_PAIRS = 8192


def touch_ends(array, key, least, largest):
    extent = array.shape
    place = [jax.random.randint(jax.random.fold_in(key, axis), (), 0, extent[axis]) for axis in range(len(extent))]
    array = array.at[tuple(place)].set(least)
    longest = extent.index(max(extent))
    place[longest] = (place[longest] + 1) % extent[longest]
    return array.at[tuple(place)].set(largest)


def steps_of(key, extent, shards, low, top_value):
    def one(dim, shards_of):
        heights = jax.random.uniform(jax.random.fold_in(jax.random.fold_in(key, 6), dim), (shards_of,), jnp.float32, low / len(shards), top_value / len(shards))
        return jnp.repeat(jnp.exp(heights), extent[dim] // shards_of).reshape((-1,) + (1,) * (len(extent) - dim - 1))

    factor_of = one(*shards[0])
    for cut in shards[1:]:
        factor_of = factor_of * one(*cut)
    return factor_of


def scatter_about(stream_key, shape, deviation, limit, shards=(), dtype=jnp.bfloat16):
    values = deviation * jax.random.normal(stream_key, shape, jnp.float32)
    if shards:
        values = values * steps_of(stream_key, shape, shards, -0.22, 0.18)
    return jnp.clip(values, -limit, limit).astype(dtype)


def setup_inputs(seed: int = 0) -> dict:
    splits = jax.random.split(jax.random.key(seed), 6)
    amplitudes = scatter_about(splits[0], (2, PANEL, PAIRS), 1.0, 6.0, ((1, 16), (2, 2)))
    integrals = scatter_about(splits[1], (2, PANEL, AO_PAIRS), (2 * PANEL) ** -0.5, 0.125, ((1, 2), (2, 16)))
    amp_screen = touch_ends((jax.random.randint(splits[2], (2, PANEL // TILE, PAIRS // TILE), 0, 4) < 3).astype(jnp.int32), jax.random.fold_in(splits[2], 1), 0, 1)
    int_screen = touch_ends((jax.random.randint(splits[3], (2, PANEL // TILE, AO_PAIRS // TILE), 0, 4) < 3).astype(jnp.int32), jax.random.fold_in(splits[3], 1), 0, 1)
    residual_in = scatter_about(splits[4], (PAIRS, AO_PAIRS), 1.0, 6.0, ((0, 2), (1, 16)), jnp.float32)
    return dict(amplitudes=amplitudes, integrals=integrals, amp_screen=amp_screen, int_screen=int_screen, residual_in=residual_in)


def reference(amplitudes, integrals, amp_screen, int_screen, residual_in):
    amp_full = jnp.repeat(jnp.repeat(amp_screen, TILE, axis=1), TILE, axis=2)
    int_full = jnp.repeat(jnp.repeat(int_screen, TILE, axis=1), TILE, axis=2)
    kept_amps = amplitudes * amp_full.astype(jnp.bfloat16)
    kept_ints = integrals * int_full.astype(jnp.bfloat16)
    first = jnp.dot(kept_amps[0].T, kept_ints[0], preferred_element_type=jnp.float32)
    second = jnp.dot(kept_amps[1].T, kept_ints[1], preferred_element_type=jnp.float32)
    return residual_in + first + second
```

```python
import functools

import jax
import jax.numpy as jnp
from jax import lax
from jax.experimental import pallas as pl
from jax.experimental.pallas import tpu as pltpu
from jax.sharding import PartitionSpec as P

TILE = 128
STEP = 256


def spread_rows(screen, first, height):
    tile_rows = (first + jnp.arange(height, dtype=jnp.int32)) // TILE
    picked = jnp.take(screen, tile_rows, axis=1)
    return jnp.repeat(picked, TILE, axis=2).astype(jnp.bfloat16)


def gathered(amplitudes, integrals, amp_screen, int_screen, residual_in):
    high, deep = amplitudes.shape[1], integrals.shape[1]
    kept_amps = amplitudes * spread_rows(amp_screen, lax.axis_index("col") * high, high)
    kept_ints = integrals * spread_rows(int_screen, lax.axis_index("row") * deep, deep)
    return residual_in + jnp.einsum(
        "pki,pkj->ij",
        lax.all_gather(kept_amps, "col", axis=1, tiled=True),
        lax.all_gather(kept_ints, "row", axis=1, tiled=True),
        preferred_element_type=jnp.float32,
    )


def chip(z, y, x):
    return (z * 2 + y) * 2 + x


def permutation(move):
    pairs = []
    for r in range(2):
        for z in range(4):
            for y in range(2):
                for x in range(2):
                    pairs.append((r * 16 + chip(z, y, x), r * 16 + chip(*move(r, z, y, x))))
    return pairs


CYCLE = (1, 3, 0, 2)
AHEAD = permutation(lambda r, z, y, x: (CYCLE[z], y, x))
BACK = permutation(lambda r, z, y, x: (CYCLE.index(z), y, x))
FIRST = permutation(lambda r, z, y, x: (z, y, 1 - x) if r == 0 else (z, 1 - y, x))
LAST = permutation(lambda r, z, y, x: (z, 1 - y, x) if r == 0 else (z, y, 1 - x))


def send(block, pairs):
    return lax.ppermute(block, ("row", "col"), pairs)


def origin(part, member, row, col):
    z, flat = col // 4, col % 4
    high, low = z // 2, z % 2
    if part == 1:
        z = (1 - low) * 2 + high
    elif part == 2:
        z = low * 2 + (1 - high)
    elif part == 3:
        z = 3 - z
    y, x = flat // 2, flat % 2
    flip_x = {0: 0, 1: 1 - row, 2: row, 3: 1}[member]
    flip_y = {0: 0, 1: row, 2: 1 - row, 3: 1}[member]
    x = x + flip_x - 2 * x * flip_x
    y = y + flip_y - 2 * y * flip_y
    return (z * 2 + y) * 2 + x


def contract_kernel(parts, row_ref, col_ref, amp_screen, int_screen, *refs):
    count = len(parts)
    blocks, mine, theirs = refs[:count], refs[count : 2 * count], refs[2 * count : 3 * count]
    total, out, left, right = refs[3 * count :]
    row, col = row_ref[0], col_ref[0]
    step = pl.program_id(0)
    height, width = blocks[0].shape[1], right.shape[1]

    @pl.when(step == 0)
    def _():
        for b, (part, member) in enumerate(parts):
            source = origin(part, member, row, col)
            tile = source * height // TILE
            here = source // 8 == row
            for p in range(2):
                rows = pl.ds((b * 2 + p) * height, height)
                for t in range(width // TILE):
                    cut = pl.ds(t * TILE, TILE)
                    keep = int_screen[p, t, tile] != 0
                    value = jnp.where(here, mine[b][p, 0, :, cut], theirs[b][p, 0, :, cut])
                    right[rows, cut] = jnp.where(keep, value, jnp.zeros_like(value))

    for b, (part, member) in enumerate(parts):
        tile = origin(part, member, row, col) * height // TILE
        for p in range(2):
            rows = pl.ds((b * 2 + p) * height, height)
            for t in range(STEP // TILE):
                cut = pl.ds(t * TILE, TILE)
                keep = amp_screen[p, tile, step * (STEP // TILE) + t] != 0
                value = blocks[b][p, :, cut]
                left[rows, cut] = jnp.where(keep, value, jnp.zeros_like(value))
    out[...] = total[...] + lax.dot_general(
        left[...], right[...], (((0,), (0,)), ((), ())), preferred_element_type=jnp.float32
    )


def contract(parts, blocks, mine, theirs, amp_screen, int_screen, total, row, col):
    count = len(parts)
    _, height, pairs = blocks[0].shape
    width = mine.shape[-1]

    def ints_map(part, member):
        return lambda i, row, col: (0, origin(part, member, row[0], col[0]) % 8, 0, 0)

    ints_specs = [pl.BlockSpec((2, 1, height, width), ints_map(*part)) for part in parts]
    total_spec = pl.BlockSpec((STEP, width), lambda i, row, col: (i, 0))
    depth = 2 * height * count
    return pl.pallas_call(
        functools.partial(contract_kernel, parts),
        out_shape=jax.ShapeDtypeStruct(total.shape, jnp.float32),
        grid_spec=pltpu.PrefetchScalarGridSpec(
            num_scalar_prefetch=2,
            grid=(pairs // STEP,),
            in_specs=[pl.BlockSpec(memory_space=pltpu.SMEM)] * 2
            + [pl.BlockSpec((2, height, STEP), lambda i, row, col: (0, 0, i))] * count
            + ints_specs * 2
            + [total_spec],
            out_specs=total_spec,
            scratch_shapes=[
                pltpu.VMEM((depth, STEP), jnp.bfloat16),
                pltpu.VMEM((depth, width), jnp.bfloat16),
            ],
        ),
        cost_estimate=pl.CostEstimate(
            flops=2 * depth * pairs * width,
            bytes_accessed=8 * pairs * width + 2 * depth * (pairs + 2 * width),
            transcendentals=0,
        ),
        compiler_params=pltpu.CompilerParams(vmem_limit_bytes=24 << 20),
    )(row, col, amp_screen, int_screen, *blocks, *[mine] * count, *[theirs] * count, total)


def neighbours(amplitudes, integrals, amp_screen, int_screen, residual_in):
    row = lax.axis_index("row").reshape(1).astype(jnp.int32)
    col = lax.axis_index("col").reshape(1).astype(jnp.int32)
    height, width = amplitudes.shape[1], integrals.shape[2]
    int_screen = jnp.transpose(int_screen, (0, 2, 1))

    ways = [amplitudes, send(amplitudes, AHEAD), send(amplitudes, BACK)]
    ways.append(send(ways[1], AHEAD))
    theirs = lax.ppermute(integrals, "row", [(0, 1), (1, 0)])
    mine = integrals.reshape(2, -1, height, width)
    theirs = theirs.reshape(2, -1, height, width)

    total = residual_in
    for part, block in enumerate(ways):
        across = send(block, FIRST)
        blocks = [block, across, send(block, LAST), send(across, LAST)]
        total = contract(
            [(part, member) for member in range(4)],
            blocks, mine, theirs, amp_screen, int_screen, total, row, col,
        )
    return total


def solution(mesh):
    placed = (
        P(None, "col", "row"),
        P(None, "row", "col"),
        P(None, None, "row"),
        P(None, None, "col"),
        P("row", "col"),
    )
    small = mesh.shape["row"] == 2 and mesh.shape["col"] == 16
    return jax.shard_map(
        neighbours if small else gathered,
        mesh=mesh, in_specs=placed, out_specs=P("row", "col"), check_vma=False,
    )
```

```python
import functools

import jax
import jax.numpy as jnp
from jax import lax
from jax.experimental import pallas as pl
from jax.experimental.pallas import tpu as pltpu
from jax.sharding import PartitionSpec as P


TILE = 128
SUBLANES = 16
STEP = 256


def spread_rows(screen, first, height):
    tile_rows = (first + jnp.arange(height, dtype=jnp.int32)) // TILE
    picked = jnp.take(screen, tile_rows, axis=1)
    return jnp.repeat(picked, TILE, axis=2).astype(jnp.bfloat16)


def gathered(amplitudes, integrals, amp_screen, int_screen, residual_in):
    high, deep = amplitudes.shape[1], integrals.shape[1]
    kept_amps = amplitudes * spread_rows(amp_screen, lax.axis_index("col") * high, high)
    kept_ints = integrals * spread_rows(int_screen, lax.axis_index("row") * deep, deep)
    return residual_in + jnp.einsum(
        "pki,pkj->ij",
        lax.all_gather(kept_amps, "col", axis=1, tiled=True),
        lax.all_gather(kept_ints, "row", axis=1, tiled=True),
        preferred_element_type=jnp.float32,
    )


def chip(z, y, x):
    return (z * 2 + y) * 2 + x


def permutation(move):
    pairs = []
    for r in range(2):
        for z in range(4):
            for y in range(2):
                for x in range(2):
                    pairs.append((r * 16 + chip(z, y, x), r * 16 + chip(*move(r, z, y, x))))
    return pairs


CYCLE = (1, 3, 0, 2)
AHEAD = permutation(lambda r, z, y, x: (CYCLE[z], y, x))
BACK = permutation(lambda r, z, y, x: (CYCLE.index(z), y, x))
FIRST = permutation(lambda r, z, y, x: (z, y, 1 - x) if r == 0 else (z, 1 - y, x))
LAST = permutation(lambda r, z, y, x: (z, 1 - y, x) if r == 0 else (z, y, 1 - x))


MOVES = {
    "F": (FIRST, lambda part, member: (part, member + 1)),
    "L": (LAST, lambda part, member: (part, member + 2)),
    "A": (AHEAD, lambda part, member: ({0: 1, 1: 3, 3: 2}[part], member)),
    "B": (BACK, lambda part, member: ({0: 2, 2: 3}[part], member)),
}
SENDS = {
    "f0": ("F", [(0, 0)]),
    "z1": ("A", [(0, 0)]),
    "g0": ("L", [(0, 0)]),
    "e0": ("L", [(0, 1)]),
    "z3": ("A", [(1, 0)]),
    "f1": ("F", [(1, 0)]),
    "f3": ("F", [(3, 0)]),
    "g1": ("L", [(1, 0)]),
    "e1": ("L", [(1, 1)]),
    "z2": ("B", [(0, 0)]),
    "fB": ("B", [(0, 1)]),
    "g2": ("L", [(2, 0)]),
    "e2": ("L", [(2, 1)]),
    "g3": ("L", [(3, 0)]),
    "e3": ("L", [(3, 1)]),
}
MEETINGS = ()
CALLS = (
    [(0, 0), (0, 1), (0, 2), (0, 3), (1, 0), (1, 1), (1, 2), (1, 3)],
    [(2, 0), (2, 1), (2, 3), (3, 0), (3, 1), (3, 2), (3, 3)],
    [(2, 2)],
)


def origin(part, member, row, col):
    z, flat = col // 4, col % 4
    high, low = z // 2, z % 2
    if part == 1:
        z = (1 - low) * 2 + high
    elif part == 2:
        z = low * 2 + (1 - high)
    elif part == 3:
        z = 3 - z
    y, x = flat // 2, flat % 2
    flip_x = {0: 0, 1: 1 - row, 2: row, 3: 1}[member]
    flip_y = {0: 0, 1: row, 2: 1 - row, 3: 1}[member]
    x = x + flip_x - 2 * x * flip_x
    y = y + flip_y - 2 * y * flip_y
    return (z * 2 + y) * 2 + x


SLOTS = [member for call in CALLS for member in call]


def prepare_kernel(
    row_ref, col_ref, amp_screen, int_screen, amps_hbm, mine_hbm, theirs, residual_hbm,
    own, ints, keep, total, mine, sems,
):
    copies = [
        pltpu.make_async_copy(mine_hbm, mine, sems.at[0]),
        pltpu.make_async_copy(amps_hbm, own, sems.at[1]),
        pltpu.make_async_copy(residual_hbm, total, sems.at[2]),
    ]
    for copy in copies:
        copy.start()
    row, col = row_ref[0], col_ref[0]
    height, pairs = own.shape[1:]
    width = mine.shape[2]
    for slot, (part, member) in enumerate(SLOTS):
        tile = origin(part, member, row, col) * height // TILE
        for p in range(2):
            rows = pl.ds((slot * 2 + p) * SUBLANES, SUBLANES)
            for t in range(pairs // TILE):
                value = jnp.full((SUBLANES, TILE), amp_screen[p, tile, t], jnp.int32)
                keep[rows, pl.ds(t * TILE, TILE)] = value.astype(jnp.bfloat16)
    copies[0].wait()
    for slot, (part, member) in enumerate(SLOTS):
        source = origin(part, member, row, col)
        tile = source * height // TILE
        here = source // 8 == row
        found = pl.ds(pl.multiple_of(source % 8 * height, height), height)
        for p in range(2):
            rows = pl.ds((slot * 2 + p) * height, height)
            for t in range(width // TILE):
                cut = pl.ds(t * TILE, TILE)
                value = jnp.where(here, mine[p, found, cut], theirs[p, found, cut])
                kept = int_screen[p, t, tile] != 0
                ints[rows, cut] = jnp.where(kept, value, jnp.zeros_like(value))
    copies[1].wait()
    copies[2].wait()


def join_kernel(*refs):
    *pieces, out, sem = refs
    copies = [
        pltpu.make_async_copy(piece, out.at[pl.ds(2 * n, 2)], sem.at[n])
        for n, piece in enumerate(pieces)
    ]
    for copy in copies:
        copy.start()
    for copy in copies:
        copy.wait()


def contract_kernel(first, places, last, met, ints, keep, total, *refs):
    count = 1 + max(which for which, _ in places)
    arrays, refs = refs[:count], refs[count + met :]
    out, left = refs[:2]
    height = arrays[0].shape[1]
    right = ints[pl.ds(first * 2 * height, left.shape[0]), :]
    copies = []
    for n in range(left.shape[1] // STEP):
        cut = pl.ds(n * STEP, STEP)
        for b, (which, place) in enumerate(places):
            for p in range(2):
                kept = keep[pl.ds(((first + b) * 2 + p) * SUBLANES, SUBLANES), cut]
                for k in range(height // SUBLANES):
                    value = arrays[which][2 * place + p, pl.ds(k * SUBLANES, SUBLANES), cut]
                    rows = pl.ds((b * 2 + p) * height + k * SUBLANES, SUBLANES)
                    left[rows, cut] = value * kept
        value = total[cut, :] + lax.dot_general(
            left[:, cut], right, (((0,), (0,)), ((), ())), preferred_element_type=jnp.float32
        )
        if last:
            done, sems = refs[2:]
            done[cut, :] = value
            copies.append(pltpu.make_async_copy(done.at[cut], out.at[cut], sems.at[n]))
            copies[-1].start()
        else:
            out[cut, :] = value
    for copy in copies:
        copy.wait()


VMEM = pl.BlockSpec(memory_space=pltpu.VMEM)
SMEM = pl.BlockSpec(memory_space=pltpu.SMEM)
HBM = pl.BlockSpec(memory_space=pltpu.HBM)


def prepare(row, col, amp_screen, int_screen, amplitudes, integrals, theirs, residual):
    panels, height, pairs = amplitudes.shape
    width, count = integrals.shape[2], panels * len(SLOTS)
    like = jax.ShapeDtypeStruct
    return pl.pallas_call(
        prepare_kernel,
        out_shape=(
            like(amplitudes.shape, jnp.bfloat16),
            like((count * height, width), jnp.bfloat16),
            like((count * SUBLANES, pairs), jnp.bfloat16),
            like(residual.shape, jnp.float32),
        ),
        in_specs=[SMEM] * 4 + [HBM, HBM, VMEM, HBM],
        out_specs=(VMEM,) * 4,
        scratch_shapes=[
            pltpu.VMEM(integrals.shape, jnp.bfloat16),
            pltpu.SemaphoreType.DMA((3,)),
        ],
        compiler_params=pltpu.CompilerParams(vmem_limit_bytes=16 << 20),
    )(row, col, amp_screen, int_screen, amplitudes, integrals, theirs, residual)


def join(pieces):
    panels, height, pairs = pieces[0].shape
    return pl.pallas_call(
        join_kernel,
        out_shape=jax.ShapeDtypeStruct((panels * len(pieces), height, pairs), jnp.bfloat16),
        in_specs=[pl.BlockSpec(memory_space=pl.ANY)] * len(pieces),
        out_specs=VMEM,
        scratch_shapes=[pltpu.SemaphoreType.DMA((len(pieces),))],
        compiler_params=pltpu.CompilerParams(vmem_limit_bytes=16 << 20),
    )(*pieces)


def contract(first, places, last, ints, keep, total, arrays, met):
    pairs, _ = total.shape
    depth = 2 * arrays[0].shape[1] * len(places)
    scratch = [pltpu.VMEM((depth, pairs), jnp.bfloat16)]
    if last:
        scratch += [
            pltpu.VMEM(total.shape, jnp.float32),
            pltpu.SemaphoreType.DMA((pairs // STEP,)),
        ]
    return pl.pallas_call(
        functools.partial(contract_kernel, first, places, last, len(met)),
        out_shape=jax.ShapeDtypeStruct(total.shape, jnp.float32),
        in_specs=[VMEM] * (3 + len(arrays)) + [HBM] * len(met),
        out_specs=HBM if last else VMEM,
        scratch_shapes=scratch,
        compiler_params=pltpu.CompilerParams(vmem_limit_bytes=16 << 20),
    )(ints, keep, total, *arrays, *met)


def in_hbm(array):
    return pltpu.with_memory_space_constraint(array, pltpu.HBM)


def neighbours(amplitudes, integrals, amp_screen, int_screen, residual_in):
    row = lax.axis_index("row").reshape(1).astype(jnp.int32)
    col = lax.axis_index("col").reshape(1).astype(jnp.int32)
    amp_screen = in_hbm(amp_screen)
    int_screen = in_hbm(jnp.transpose(int_screen, (0, 2, 1)))
    theirs = lax.ppermute(integrals, "row", [(0, 1), (1, 0)])
    own, ints, keep, total = prepare(
        row, col, amp_screen, int_screen,
        in_hbm(amplitudes), in_hbm(integrals), theirs, in_hbm(residual_in),
    )
    arrays, found = {((0, 0),): amplitudes}, {(0, 0): (((0, 0),), 0)}
    met = []
    for name in MEETINGS:
        token = met[-1] if met else amp_screen
        met.append(lax.ppermute(token, "row", [(0, 1), (1, 0)]))
    pending = dict(SENDS)
    while pending:
        for name, (way, members) in list(pending.items()):
            members = tuple(members)
            if not all(member in found for member in members):
                continue
            del pending[name]
            if members not in arrays:
                pieces = [arrays[(member,)] for member in members]
                arrays[members] = join(pieces)
            pairs, move = MOVES[way]
            moved = tuple(move(*member) for member in members)
            arrays[moved] = lax.ppermute(arrays[members], ("row", "col"), pairs)
            for place, member in enumerate(moved):
                found[member] = (moved, place)
    arrays[((0, 0),)] = own
    for n, parts in enumerate(CALLS):
        names = list(dict.fromkeys(found[part][0] for part in parts))
        places = [(names.index(found[part][0]), found[part][1]) for part in parts]
        total = contract(
            SLOTS.index(parts[0]), places, n == len(CALLS) - 1, ints, keep, total,
            [arrays[name] for name in names], met if n == 0 else [],
        )
    return total


def solution(mesh):
    placed = (
        P(None, "col", "row"),
        P(None, "row", "col"),
        P(None, None, "row"),
        P(None, None, "col"),
        P("row", "col"),
    )
    small = mesh.shape["row"] == 2 and mesh.shape["col"] == 16
    return jax.shard_map(
        neighbours if small else gathered,
        mesh=mesh, in_specs=placed, out_specs=P("row", "col"), check_vma=False,
    )
```

```python
import functools

import jax
import jax.numpy as jnp
from jax import lax
from jax.experimental import pallas as pl
from jax.experimental.pallas import tpu as pltpu
from jax.sharding import PartitionSpec as P


TILE = 128
SUBLANES = 16
STEP = 256


def spread_rows(screen, first, height):
    tile_rows = (first + jnp.arange(height, dtype=jnp.int32)) // TILE
    picked = jnp.take(screen, tile_rows, axis=1)
    return jnp.repeat(picked, TILE, axis=2).astype(jnp.bfloat16)


def gathered(amplitudes, integrals, amp_screen, int_screen, residual_in):
    high, deep = amplitudes.shape[1], integrals.shape[1]
    kept_amps = amplitudes * spread_rows(amp_screen, lax.axis_index("col") * high, high)
    kept_ints = integrals * spread_rows(int_screen, lax.axis_index("row") * deep, deep)
    return residual_in + jnp.einsum(
        "pki,pkj->ij",
        lax.all_gather(kept_amps, "col", axis=1, tiled=True),
        lax.all_gather(kept_ints, "row", axis=1, tiled=True),
        preferred_element_type=jnp.float32,
    )


def chip(z, y, x):
    return (z * 2 + y) * 2 + x


def permutation(move):
    pairs = []
    for r in range(2):
        for z in range(4):
            for y in range(2):
                for x in range(2):
                    pairs.append((r * 16 + chip(z, y, x), r * 16 + chip(*move(r, z, y, x))))
    return pairs


CYCLE = (1, 3, 0, 2)
AHEAD = permutation(lambda r, z, y, x: (CYCLE[z], y, x))
BACK = permutation(lambda r, z, y, x: (CYCLE.index(z), y, x))
FIRST = permutation(lambda r, z, y, x: (z, y, 1 - x) if r == 0 else (z, 1 - y, x))
LAST = permutation(lambda r, z, y, x: (z, 1 - y, x) if r == 0 else (z, y, 1 - x))


MOVES = {
    "F": (FIRST, lambda part, member: (part, member + 1)),
    "L": (LAST, lambda part, member: (part, member + 2)),
    "A": (AHEAD, lambda part, member: ({0: 1, 1: 3, 3: 2}[part], member)),
    "B": (BACK, lambda part, member: ({0: 2, 2: 3}[part], member)),
}
SENDS = {
    "f0": ("F", [(0, 0)]),
    "z1": ("A", [(0, 0)]),
    "g0": ("L", [(0, 0)]),
    "e0": ("L", [(0, 1)]),
    "z3": ("A", [(1, 0)]),
    "f1": ("F", [(1, 0)]),
    "f3": ("F", [(3, 0)]),
    "g1": ("L", [(1, 0)]),
    "e1": ("L", [(1, 1)]),
    "z2": ("B", [(0, 0)]),
    "fB": ("B", [(0, 1)]),
    "g2": ("L", [(2, 0, 1)]),
    "e2": ("L", [(2, 1)]),
    "g3": ("L", [(3, 0)]),
    "e3": ("L", [(3, 1)]),
    "hB": ("B", [(0, 2, 0)]),
}
MEETINGS = ()
CALLS = (
    [(0, 0), (0, 1), (0, 2), (0, 3), (1, 0), (1, 1), (1, 2), (1, 3)],
    [(2, 0), (2, 1), (3, 0), (3, 1), (3, 2), (3, 3)],
    [(2, 2), (2, 3)],
)


def origin(part, member, row, col):
    z, flat = col // 4, col % 4
    high, low = z // 2, z % 2
    if part == 1:
        z = (1 - low) * 2 + high
    elif part == 2:
        z = low * 2 + (1 - high)
    elif part == 3:
        z = 3 - z
    y, x = flat // 2, flat % 2
    flip_x = {0: 0, 1: 1 - row, 2: row, 3: 1}[member]
    flip_y = {0: 0, 1: row, 2: 1 - row, 3: 1}[member]
    x = x + flip_x - 2 * x * flip_x
    y = y + flip_y - 2 * y * flip_y
    return (z * 2 + y) * 2 + x


SLOTS = [member for call in CALLS for member in call]


def prepare_kernel(
    row_ref, col_ref, amp_screen, int_screen, amps_hbm, mine_hbm, theirs, residual_hbm,
    own, ints, keep, total, mine, sems,
):
    copies = [
        pltpu.make_async_copy(mine_hbm, mine, sems.at[0]),
        pltpu.make_async_copy(amps_hbm, own, sems.at[1]),
        pltpu.make_async_copy(residual_hbm, total, sems.at[2]),
    ]
    for copy in copies:
        copy.start()
    row, col = row_ref[0], col_ref[0]
    height, pairs = own.shape[1:]
    width = mine.shape[2]
    for slot, (part, member) in enumerate(SLOTS):
        tile = origin(part, member, row, col) * height // TILE
        for p in range(2):
            rows = pl.ds((slot * 2 + p) * SUBLANES, SUBLANES)
            for t in range(pairs // TILE):
                value = jnp.full((SUBLANES, TILE), amp_screen[p, tile, t], jnp.int32)
                keep[rows, pl.ds(t * TILE, TILE)] = value.astype(jnp.bfloat16)
    copies[0].wait()
    for slot, (part, member) in enumerate(SLOTS):
        source = origin(part, member, row, col)
        tile = source * height // TILE
        here = source // 8 == row
        found = pl.ds(pl.multiple_of(source % 8 * height, height), height)
        for p in range(2):
            rows = pl.ds((slot * 2 + p) * height, height)
            for t in range(width // TILE):
                cut = pl.ds(t * TILE, TILE)
                value = jnp.where(here, mine[p, found, cut], theirs[p, found, cut])
                kept = int_screen[p, t, tile] != 0
                ints[rows, cut] = jnp.where(kept, value, jnp.zeros_like(value))
    copies[1].wait()
    copies[2].wait()


def join_kernel(cuts, *refs):
    *pieces, out, sem = refs
    copies, filled = [], 0
    for n, (start, size) in enumerate(cuts):
        source, target = pieces[n].at[pl.ds(start, size)], out.at[pl.ds(filled, size)]
        copies.append(pltpu.make_async_copy(source, target, sem.at[n]))
        filled += size
    for copy in copies:
        copy.start()
    for copy in copies:
        copy.wait()


def contract_kernel(first, places, last, met, ints, keep, total, *refs):
    count = 1 + max(which for which, _ in places)
    arrays, refs = refs[:count], refs[count + met :]
    out, left = refs[:2]
    height = arrays[0].shape[1]
    right = ints[pl.ds(first * 2 * height, left.shape[0]), :]
    copies = []
    for n in range(left.shape[1] // STEP):
        cut = pl.ds(n * STEP, STEP)
        for b, (which, place) in enumerate(places):
            kept = keep[pl.ds((first * 2 + b) * SUBLANES, SUBLANES), cut]
            for k in range(height // SUBLANES):
                value = arrays[which][place, pl.ds(k * SUBLANES, SUBLANES), cut]
                left[pl.ds(b * height + k * SUBLANES, SUBLANES), cut] = value * kept
        value = total[cut, :] + lax.dot_general(
            left[:, cut], right, (((0,), (0,)), ((), ())), preferred_element_type=jnp.float32
        )
        if last:
            done, sems = refs[2:]
            done[cut, :] = value
            copies.append(pltpu.make_async_copy(done.at[cut], out.at[cut], sems.at[n]))
            copies[-1].start()
        else:
            out[cut, :] = value
    for copy in copies:
        copy.wait()


VMEM = pl.BlockSpec(memory_space=pltpu.VMEM)
SMEM = pl.BlockSpec(memory_space=pltpu.SMEM)
HBM = pl.BlockSpec(memory_space=pltpu.HBM)


def prepare(row, col, amp_screen, int_screen, amplitudes, integrals, theirs, residual):
    panels, height, pairs = amplitudes.shape
    width, count = integrals.shape[2], panels * len(SLOTS)
    like = jax.ShapeDtypeStruct
    return pl.pallas_call(
        prepare_kernel,
        out_shape=(
            like(amplitudes.shape, jnp.bfloat16),
            like((count * height, width), jnp.bfloat16),
            like((count * SUBLANES, pairs), jnp.bfloat16),
            like(residual.shape, jnp.float32),
        ),
        in_specs=[SMEM] * 4 + [HBM, HBM, VMEM, HBM],
        out_specs=(VMEM,) * 4,
        scratch_shapes=[
            pltpu.VMEM(integrals.shape, jnp.bfloat16),
            pltpu.SemaphoreType.DMA((3,)),
        ],
        compiler_params=pltpu.CompilerParams(vmem_limit_bytes=16 << 20),
    )(row, col, amp_screen, int_screen, amplitudes, integrals, theirs, residual)


def join(pieces):
    arrays = [array for array, _, _ in pieces]
    cuts = [(start, size) for _, start, size in pieces]
    shape = (sum(size for _, size in cuts),) + arrays[0].shape[1:]
    return pl.pallas_call(
        functools.partial(join_kernel, cuts),
        out_shape=jax.ShapeDtypeStruct(shape, jnp.bfloat16),
        in_specs=[pl.BlockSpec(memory_space=pl.ANY)] * len(pieces),
        out_specs=VMEM,
        scratch_shapes=[pltpu.SemaphoreType.DMA((len(pieces),))],
        compiler_params=pltpu.CompilerParams(vmem_limit_bytes=16 << 20),
    )(*arrays)


def contract(first, places, last, ints, keep, total, arrays, met):
    pairs, _ = total.shape
    depth = arrays[0].shape[1] * len(places)
    scratch = [pltpu.VMEM((depth, pairs), jnp.bfloat16)]
    if last:
        scratch += [
            pltpu.VMEM(total.shape, jnp.float32),
            pltpu.SemaphoreType.DMA((pairs // STEP,)),
        ]
    return pl.pallas_call(
        functools.partial(contract_kernel, first, places, last, len(met)),
        out_shape=jax.ShapeDtypeStruct(total.shape, jnp.float32),
        in_specs=[VMEM] * (3 + len(arrays)) + [HBM] * len(met),
        out_specs=HBM if last else VMEM,
        scratch_shapes=scratch,
        compiler_params=pltpu.CompilerParams(vmem_limit_bytes=16 << 20),
    )(ints, keep, total, *arrays, *met)


def in_hbm(array):
    return pltpu.with_memory_space_constraint(array, pltpu.HBM)


def neighbours(amplitudes, integrals, amp_screen, int_screen, residual_in):
    row = lax.axis_index("row").reshape(1).astype(jnp.int32)
    col = lax.axis_index("col").reshape(1).astype(jnp.int32)
    amp_screen = in_hbm(amp_screen)
    int_screen = in_hbm(jnp.transpose(int_screen, (0, 2, 1)))
    theirs = lax.ppermute(integrals, "row", [(0, 1), (1, 0)])
    own, ints, keep, total = prepare(
        row, col, amp_screen, int_screen,
        in_hbm(amplitudes), in_hbm(integrals), theirs, in_hbm(residual_in),
    )
    arrays, found = {((0, 0),): amplitudes}, {(0, 0): (((0, 0),), 0)}
    met = []
    for name in MEETINGS:
        token = met[-1] if met else amp_screen
        met.append(lax.ppermute(token, "row", [(0, 1), (1, 0)]))
    pending = dict(SENDS)
    while pending:
        for name, (way, members) in list(pending.items()):
            members = tuple(members)
            if not all(member[:2] in found for member in members):
                continue
            del pending[name]
            if members not in arrays:
                pieces = []
                for member in members:
                    which, start = found[member[:2]]
                    start, size = start + sum(member[2:]), 4 - len(member)
                    pieces.append((arrays[which], start, size))
                arrays[members] = join(pieces)
            pairs, move = MOVES[way]
            moved = tuple(move(*member[:2]) + member[2:] for member in members)
            arrays[moved] = lax.ppermute(arrays[members], ("row", "col"), pairs)
            start = 0
            for member in moved:
                found[member] = (moved, start)
                start += 4 - len(member)
    arrays[((0, 0),)] = own
    for n, parts in enumerate(CALLS):
        rows = []
        for part in parts:
            for p in range(2):
                which, start = found.get(part + (p,)) or found[part]
                rows.append((which, start if part + (p,) in found else start + p))
        names = list(dict.fromkeys(which for which, _ in rows))
        places = [(names.index(which), start) for which, start in rows]
        total = contract(
            SLOTS.index(parts[0]), places, n == len(CALLS) - 1, ints, keep, total,
            [arrays[name] for name in names], met if n == 0 else [],
        )
    return total


def solution(mesh):
    placed = (
        P(None, "col", "row"),
        P(None, "row", "col"),
        P(None, None, "row"),
        P(None, None, "col"),
        P("row", "col"),
    )
    small = mesh.shape["row"] == 2 and mesh.shape["col"] == 16
    return jax.shard_map(
        neighbours if small else gathered,
        mesh=mesh, in_specs=placed, out_specs=P("row", "col"), check_vma=False,
    )
```
